256 devices in a mesh: rows: 64 (over y, x_lo, z), cols: 4 (over x_hi, core).
Axes of the slice: x: 4 (x_hi: 2, x_lo: 2; x = x_hi * 2 + x_lo), y: 4, z: 8, core: 2. Of those that a mesh axis runs over, the one named last changes fastest.
Arguments:
- right_vecs: bfloat16 [2, 131072, 512], P(None, 'rows', 'cols'), may hold values from -6 to 6
- left_vecs: bfloat16 [2, 131072, 512], P(None, 'rows', 'cols'), may hold values from -0.046875 to 0.046875
- dip_blocks: bfloat16 [1024, 8, 2, 128, 128], P('rows'), may hold values from -0.125 to 0.125
- block_cols: int32 [1024, 8], P('rows'), may hold values from 0 to 1023, as said below
- block_counts: int32 [1024], P('rows'), may hold values from 1 to 8, as said below
Outputs:
- coupling: float32 [4, 128, 2, 512], P(None, 'rows')
The draws below stay inside these ranges and needn't reach their ends.
Inputs may be any that keep to these rules, and one draw needn't show every extreme that they name: Block row r's columns lie within 16 blocks of r: |block_cols[r, j] - r| <= 16, slots at or past block_counts[r] included; such slots are not used. Slots in use fill the first block_counts[r] slots of a block row.
All inputs are finite; a program needn't handle non-finite values.
Results may differ from the reference program's by a relative error of at most 0.0029.
Values may be sent and summed in bfloat16 or wider, within the bound.
No kernel may reach another device: no remote copies, remote signals or barrier semaphores. Data moves between devices by JAX's collectives and lax.ppermute only.
A program may use at most 128 MiB of HBM per device.

```python
import jax
import jax.numpy as jnp
from jax import lax

K = 512
BS = 128
MAXB = 8
BPD = 16
NBR = 1024
NR = 131072
KG = 128


def draw_block_cols(key, part):
    row_ids = jnp.arange(NBR, dtype=jnp.int32)
    offsets = jax.random.randint(key, (NBR, MAXB), -BPD, BPD + 1, dtype=jnp.int32)
    return jnp.clip(row_ids[:, None] + offsets, 0, NBR - 1).astype(jnp.int32)


def draw_block_counts(key, part):
    key_heavy, key_pick, key_high, key_low = jax.random.split(jax.random.fold_in(key, 7), 4)
    groups = NBR // BPD
    heavy = jax.random.randint(key_heavy, (groups,), 0, 4, dtype=jnp.int32) == 0
    chosen = jax.random.randint(key_pick, (), 0, groups, dtype=jnp.int32)
    heavy = heavy.at[chosen].set(True)
    heavy_rows = jnp.repeat(heavy, BPD)
    high = jax.random.randint(key_high, (NBR,), MAXB // 2, MAXB + 1, dtype=jnp.int32)
    low = jax.random.randint(key_low, (NBR,), 1, 3, dtype=jnp.int32)
    counts = jnp.where(heavy_rows, high, low)
    return counts.at[chosen * BPD].set(MAXB).astype(jnp.int32)


def raised(drawn, own_key, source, target, parts, factor):
    owner, partner = [(jnp.arange(drawn.shape[position]) // (drawn.shape[position] // parts)).reshape([-1 if axis == position else 1 for axis in range(drawn.ndim)]) for position in (source, target)]
    chosen = jax.random.permutation(own_key, parts)[partner]
    strong = (owner == chosen) | (owner == (partner + parts // 2) % parts)
    return jnp.where(strong, factor * drawn, drawn)


def block_levels(stream_key, shape, cuts, low, high):
    def one(axis_at, parts):
        steps = jax.random.uniform(jax.random.fold_in(jax.random.fold_in(stream_key, 6), axis_at), (parts,), jnp.float32, low / len(cuts), high / len(cuts))
        return jnp.repeat(jnp.exp(steps), shape[axis_at] // parts).reshape((-1,) + (1,) * (len(shape) - axis_at - 1))

    gain = one(*cuts[0])
    for cut in cuts[1:]:
        gain = gain * one(*cut)
    return gain


def normal_values(stream_key, dims, width, limit, shards=(), held_as=jnp.bfloat16):
    factor_of = block_levels(stream_key, dims, shards, -0.22, 0.18) if shards else 1.0
    array = jax.random.normal(stream_key, dims, jnp.float32) * width * factor_of
    return jnp.minimum(jnp.maximum(array, -limit), limit).astype(held_as)


def noise_with(own_key, dims, width, bound, cuts, heavy, held_as=jnp.bfloat16):
    entries = width * jax.random.normal(own_key, dims, jnp.float32)
    if cuts:
        entries = entries * block_levels(own_key, dims, cuts, -0.22, 0.18)
    return jnp.clip(raised(entries, jax.random.fold_in(own_key, 3), *heavy), -bound, bound).astype(held_as)


def setup_inputs(seed: int = 0) -> dict:
    key_of = jax.random.split(jax.random.key(seed), 6)
    return {
        "right_vecs": normal_values(key_of[0], (2, NR, K), 1.0, 6.0, ((1, 64), (2, 4))),
        "left_vecs": noise_with(key_of[1], (2, NR, K), NR ** -0.5, 0.046875, ((1, 64), (2, 4)), (1, 2, 64, 4.0)),
        "dip_blocks": normal_values(key_of[2], (NBR, MAXB, 2, BS, BS), (2 * MAXB * BS) ** -0.5, 0.125, ((0, 64),)),
        "block_cols": draw_block_cols(jax.random.fold_in(key_of[5], 71), 0),
        "block_counts": draw_block_counts(jax.random.fold_in(key_of[5], 71), 0),
    }


def reference(right_vecs, left_vecs, dip_blocks, block_cols, block_counts):
    blocked = right_vecs.reshape(2, NBR, BS, K)
    slot_ids = jnp.arange(MAXB, dtype=jnp.int32)

    def one_row(args):
        mats, cols, count = args
        vecs = jnp.take(blocked, cols, axis=1).astype(jnp.float32)
        valid = (slot_ids < count)[None, :, None, None]
        vecs = jnp.where(valid, vecs, jnp.zeros_like(vecs))
        mats = mats.astype(jnp.float32)
        real_part = jnp.einsum("jpq,jqk->pk", mats[:, 0], vecs[0]) - jnp.einsum("jpq,jqk->pk", mats[:, 1], vecs[1])
        imag_part = jnp.einsum("jpq,jqk->pk", mats[:, 0], vecs[1]) + jnp.einsum("jpq,jqk->pk", mats[:, 1], vecs[0])
        return jnp.stack([real_part, imag_part]).astype(jnp.bfloat16)

    rows_out = lax.map(one_row, (dip_blocks, block_cols, block_counts))
    image = jnp.transpose(rows_out, (1, 0, 2, 3)).reshape(2, NR, K)
    left_re = left_vecs[0].T
    left_im = left_vecs[1].T
    real_part = jnp.dot(left_re, image[0], preferred_element_type=jnp.float32) + jnp.dot(left_im, image[1], preferred_element_type=jnp.float32)
    imag_part = jnp.dot(left_re, image[1], preferred_element_type=jnp.float32) - jnp.dot(left_im, image[0], preferred_element_type=jnp.float32)
    return jnp.stack([real_part, imag_part], axis=1).reshape(K // KG, KG, 2, K)
```

```python
import jax
import jax.numpy as jnp
from jax import lax
from jax.experimental import pallas as pl
from jax.experimental.pallas import tpu as pltpu
from jax.sharding import PartitionSpec as P


ROWS_STEP = 2


def whole(shape):
    return pl.BlockSpec(shape, lambda i, *_: (0,) * len(shape))


def params(mib):
    return pltpu.CompilerParams(dimension_semantics=("arbitrary",), vmem_limit_bytes=mib * 1024 * 1024)


def build_weights(weights, ref, base):
    _, blocks, size, width = ref.shape

    def build(i, carry):
        real = ref[0, i]
        imag = ref[1, i]
        weights[base + i, :size, :width] = real
        weights[base + i, :size, width:] = imag
        weights[base + i, size:, :width] = -imag
        weights[base + i, size:, width:] = real
        return carry

    lax.fori_loop(0, blocks, build, 0)


def add_slots(acc, k, row, cols_ref, counts_ref, dip_ref, weights, pick):
    def slot(j, carry):
        used, at = pick(cols_ref[row, j])

        @pl.when(used)
        def _():
            lhs = jnp.concatenate([dip_ref[k, j, 0], dip_ref[k, j, 1]], axis=1)
            acc[k] += jnp.dot(lhs, weights[at], preferred_element_type=jnp.float32)

        return carry

    lax.fori_loop(0, counts_ref[row], slot, 0)


def own_kernel(cols_ref, counts_ref, own_ref, dip_ref, acc_ref, weights):
    step = pl.program_id(0)
    blocks = own_ref.shape[1]

    @pl.when(step == 0)
    def _():
        build_weights(weights, own_ref, 0)

    def pick(col):
        return (col >= blocks) & (col < 2 * blocks), col - blocks

    acc_ref[...] = jnp.zeros_like(acc_ref)
    for k in range(ROWS_STEP):
        add_slots(acc_ref, k, step * ROWS_STEP + k, cols_ref, counts_ref, dip_ref, weights, pick)


def halo_kernel(cols_ref, counts_ref, low_ref, high_ref, dip_ref, acc_in_ref, image_ref, weights, acc):
    step = pl.program_id(0)
    blocks = low_ref.shape[1]

    @pl.when(step == 0)
    def _():
        build_weights(weights, low_ref, 0)
        build_weights(weights, high_ref, blocks)

    def pick(col):
        return (col < blocks) | (col >= 2 * blocks), jnp.where(col < blocks, col, col - blocks)

    acc[...] = acc_in_ref[...]
    for k in range(ROWS_STEP):
        add_slots(acc, k, step * ROWS_STEP + k, cols_ref, counts_ref, dip_ref, weights, pick)
    image_ref[...] = acc[...].astype(image_ref.dtype)


def specs(dips, width):
    _, slots, _, size, _ = dips.shape
    dip = pl.BlockSpec((ROWS_STEP, slots, 2, size, size), lambda i, *_: (i, 0, 0, 0, 0))
    acc = pl.BlockSpec((ROWS_STEP, size, 2 * width), lambda i, *_: (i, 0, 0))
    return dip, acc


def own_products(cols, counts, own, dips):
    rows, _, _, size, _ = dips.shape
    width = own.shape[-1]
    dip, acc = specs(dips, width)
    return pl.pallas_call(
        own_kernel,
        out_shape=jax.ShapeDtypeStruct((rows, size, 2 * width), jnp.float32),
        grid_spec=pltpu.PrefetchScalarGridSpec(
            num_scalar_prefetch=2,
            grid=(rows // ROWS_STEP,),
            in_specs=[whole(own.shape), dip],
            out_specs=acc,
            scratch_shapes=[pltpu.VMEM((rows, 2 * size, 2 * width), jnp.bfloat16)],
        ),
        compiler_params=params(16),
        cost_estimate=pl.CostEstimate(flops=1_000_000_000, bytes_accessed=11_000_000, transcendentals=0),
    )(cols, counts, own, dips)


def halo_products(cols, counts, low, high, dips, acc_in):
    rows, _, _, size, _ = dips.shape
    width = low.shape[-1]
    dip, acc = specs(dips, width)
    return pl.pallas_call(
        halo_kernel,
        out_shape=jax.ShapeDtypeStruct((rows, size, 2 * width), jnp.bfloat16),
        grid_spec=pltpu.PrefetchScalarGridSpec(
            num_scalar_prefetch=2,
            grid=(rows // ROWS_STEP,),
            in_specs=[whole(low.shape), whole(high.shape), dip, acc],
            out_specs=acc,
            scratch_shapes=[
                pltpu.VMEM((2 * rows, 2 * size, 2 * width), jnp.bfloat16),
                pltpu.VMEM((ROWS_STEP, size, 2 * width), jnp.float32),
            ],
        ),
        compiler_params=params(24),
        cost_estimate=pl.CostEstimate(flops=1_000_000_000, bytes_accessed=12_000_000, transcendentals=0),
    )(cols, counts, low, high, dips, acc_in)


def project_kernel(left_ref, image_ref, other_ref, out_ref, total):
    step = pl.program_id(0)
    width = left_ref.shape[-1]
    chunks, each2, _ = out_ref.shape
    each = each2 // 2

    @pl.when(step == 0)
    def _():
        total[...] = jnp.zeros_like(total)

    images = jnp.concatenate([image_ref[...], other_ref[...]], axis=1)
    for part in range(2):
        total[part] += lax.dot_general(
            left_ref[part], images, (((0,), (0,)), ((), ())), preferred_element_type=jnp.float32
        )

    @pl.when(step == pl.num_programs(0) - 1)
    def _():
        for t in range(2):
            re = slice(2 * t * width, (2 * t + 1) * width)
            im = slice((2 * t + 1) * width, (2 * t + 2) * width)
            to = slice(t * width, (t + 1) * width)
            real = total[0, :, re] + total[1, :, im]
            imag = total[0, :, im] - total[1, :, re]
            out_ref[:, :each, to] = real.reshape(chunks, each, width)
            out_ref[:, each:, to] = imag.reshape(chunks, each, width)


def project(left, image, other, chunks):
    _, span, width = left.shape
    each = width // chunks
    tile = min(512, span)
    return pl.pallas_call(
        project_kernel,
        out_shape=jax.ShapeDtypeStruct((chunks, 2 * each, 2 * width), jnp.float32),
        grid_spec=pl.GridSpec(
            grid=(span // tile,),
            in_specs=[
                pl.BlockSpec((2, tile, width), lambda i: (0, i, 0)),
                pl.BlockSpec((tile, 2 * width), lambda i: (i, 0)),
                pl.BlockSpec((tile, 2 * width), lambda i: (i, 0)),
            ],
            out_specs=whole((chunks, 2 * each, 2 * width)),
            scratch_shapes=[pltpu.VMEM((2, width, 4 * width), jnp.float32)],
        ),
        compiler_params=params(16),
        cost_estimate=pl.CostEstimate(flops=600_000_000, bytes_accessed=3_500_000, transcendentals=0),
    )(left, image, other)


def local(right_vecs, left_vecs, dip_blocks, block_cols, block_counts):
    parts, span, width = right_vecs.shape
    blocks, _, _, size, _ = dip_blocks.shape
    n_rows = lax.axis_size("rows")
    n_cols = lax.axis_size("cols")
    each = width // n_rows
    forward = [(i, i + 1) for i in range(n_rows - 1)]
    backward = [(j, i) for i, j in forward]
    blocked = lambda x: x.reshape(parts, blocks, size, width)
    local_cols = block_cols - (lax.axis_index("rows") - 1) * blocks
    low = lax.ppermute(right_vecs, "rows", forward)
    high = lax.ppermute(right_vecs, "rows", backward)
    across = lax.ppermute(left_vecs, "cols", [(i, i ^ 2) for i in range(n_cols)])
    acc = own_products(local_cols, block_counts, blocked(right_vecs), dip_blocks)
    image = halo_products(local_cols, block_counts, blocked(low), blocked(high), dip_blocks, acc)
    image = image.reshape(span, 2 * width)
    other = lax.ppermute(image, "cols", [(i, i ^ 1) for i in range(n_cols)])
    near = project(left_vecs, image, other, n_rows)
    far = project(across, image, other, n_rows)
    partial = jnp.concatenate([near, far], axis=1).astype(jnp.bfloat16)
    received = lax.all_to_all(partial, "rows", 0, 0, tiled=True)
    share = jnp.sum(received.astype(jnp.float32), axis=0).reshape(2, parts, each, 2, width)
    me = lax.axis_index("cols")
    share = jnp.where((me & 2) > 0, share[::-1], share)
    share = jnp.where((me & 1) > 0, share[:, :, :, ::-1], share)
    out = lax.all_gather(share.reshape(2 * parts * each, 2 * width), "cols", axis=0)
    out = out.reshape(2, 2, 2, parts, each, 2, width)
    return out.transpose(2, 1, 4, 3, 0, 5, 6).reshape(n_cols, each, parts, n_cols * width)


def solution(mesh):
    in_specs = (
        P(None, "rows", "cols"),
        P(None, "rows", "cols"),
        P("rows", None, None, None, None),
        P("rows", None),
        P("rows"),
    )
    out_specs = P(None, "rows", None, None)
    return jax.shard_map(local, mesh=mesh, in_specs=in_specs, out_specs=out_specs, check_vma=False)
```

```python
import jax
import jax.numpy as jnp
from jax import lax
from jax.experimental import pallas as pl
from jax.experimental.pallas import tpu as pltpu
from jax.sharding import PartitionSpec as P


UNROLL = 4
TILE = 256
LINE = 8
TAIL_TILES = 3


def build_weights(weights, ref, base):
    _, blocks, size, width = ref.shape

    def build(i, carry):
        real = ref[0, i]
        imag = ref[1, i]
        weights[base + i, :size, :width] = real
        weights[base + i, :size, width:] = imag
        weights[base + i, size:, :width] = -imag
        weights[base + i, size:, width:] = real
        return carry

    lax.fori_loop(0, blocks, build, 0)


def add_slots(acc, dip_ref, weights, list_ref, count):
    slots = dip_ref.shape[1]
    n_weights = weights.shape[0]

    def group(g, carry):
        for u in range(UNROLL):
            code = list_ref[g * UNROLL + u]
            slot = code // n_weights
            row = slot // slots
            at = code % n_weights
            lhs = jnp.concatenate([dip_ref[row, slot % slots, 0], dip_ref[row, slot % slots, 1]], axis=1)
            acc[row] += jnp.dot(lhs, weights[at], preferred_element_type=jnp.float32)
        return carry

    lax.fori_loop(0, count // UNROLL, group, 0)

    def one(i, carry):
        code = list_ref[i]
        slot = code // n_weights
        row = slot // slots
        at = code % n_weights
        lhs = jnp.concatenate([dip_ref[row, slot % slots, 0], dip_ref[row, slot % slots, 1]], axis=1)
        acc[row] += jnp.dot(lhs, weights[at], preferred_element_type=jnp.float32)
        return carry

    lax.fori_loop(count // UNROLL * UNROLL, count, one, 0)


def own_kernel(
    cols_ref, counts_ref, own_ref, dip_ref, acc_ref, low_list, low_count, high_list, high_count, weights, own_list
):
    rows, slots = dip_ref.shape[:2]
    blocks = own_ref.shape[1]
    build_weights(weights, own_ref, 0)
    acc_ref[...] = jnp.zeros_like(acc_ref)

    def by_row(row, carry):
        def by_slot(j, carry):
            n_low, n_own, n_high = carry
            col = cols_ref[row, j]
            slot = row * slots + j
            is_low = col < blocks
            is_high = col >= 2 * blocks
            is_own = jnp.logical_not(is_low | is_high)

            @pl.when(is_low)
            def _():
                low_list[n_low] = slot * blocks + col

            @pl.when(is_own)
            def _():
                own_list[n_own] = slot * blocks + col - blocks

            @pl.when(is_high)
            def _():
                high_list[n_high] = slot * blocks + col - 2 * blocks

            one = lambda x: x.astype(jnp.int32)
            return n_low + one(is_low), n_own + one(is_own), n_high + one(is_high)

        return lax.fori_loop(0, counts_ref[row], by_slot, carry)

    n_low, n_own, n_high = lax.fori_loop(0, rows, by_row, (jnp.int32(0),) * 3)
    low_count[0] = n_low
    high_count[0] = n_high
    add_slots(acc_ref, dip_ref, weights, own_list, n_own)


def side_kernel(list_ref, count_ref, side_ref, dip_ref, acc_in_ref, out_ref, weights, *scratch):
    build_weights(weights, side_ref, 0)
    acc = scratch[0] if scratch else out_ref
    acc[...] = acc_in_ref[...]
    add_slots(acc, dip_ref, weights, list_ref, count_ref[0])
    if scratch:
        out_ref[...] = acc[...].astype(out_ref.dtype)


def own_products(cols, counts, own, dips):
    rows, slots, _, size, _ = dips.shape
    width = own.shape[-1]
    smem = pl.BlockSpec(memory_space=pltpu.SMEM)
    vmem = pl.BlockSpec(memory_space=pltpu.VMEM)
    slot_list = jax.ShapeDtypeStruct((rows * slots,), jnp.int32)
    one = jax.ShapeDtypeStruct((1,), jnp.int32)
    return pl.pallas_call(
        own_kernel,
        out_shape=(jax.ShapeDtypeStruct((rows, size, 2 * width), jnp.float32), slot_list, one, slot_list, one),
        in_specs=[smem, smem, vmem, vmem],
        out_specs=(vmem, smem, smem, smem, smem),
        scratch_shapes=[
            pltpu.VMEM((rows, 2 * size, 2 * width), jnp.bfloat16),
            pltpu.SMEM((rows * slots,), jnp.int32),
        ],
        compiler_params=pltpu.CompilerParams(vmem_limit_bytes=16 * 1024 * 1024),
        cost_estimate=pl.CostEstimate(flops=1_000_000_000, bytes_accessed=11_000_000, transcendentals=0),
    )(cols, counts, own, dips)


def side_products(slot_list, count, side, dips, acc_in, last):
    rows, _, _, size, _ = dips.shape
    width = side.shape[-1]
    smem = pl.BlockSpec(memory_space=pltpu.SMEM)
    vmem = pl.BlockSpec(memory_space=pltpu.VMEM)
    shape = (rows, size, 2 * width)
    scratch = [pltpu.VMEM((rows, 2 * size, 2 * width), jnp.bfloat16)]
    if last:
        scratch.append(pltpu.VMEM(shape, jnp.float32))
    return pl.pallas_call(
        side_kernel,
        out_shape=jax.ShapeDtypeStruct(shape, jnp.bfloat16 if last else jnp.float32),
        in_specs=[smem, smem, vmem, vmem, vmem],
        out_specs=vmem,
        scratch_shapes=scratch,
        compiler_params=pltpu.CompilerParams(vmem_limit_bytes=16 * 1024 * 1024),
        cost_estimate=pl.CostEstimate(flops=500_000_000, bytes_accessed=12_000_000, transcendentals=0),
    )(slot_list, count, side, dips, acc_in)


def add_tiles(total, left_of, image_ref, other_ref, first, count):
    def tile(i, carry):
        mine = pl.ds(pl.multiple_of(i * TILE, TILE), TILE)
        at = pl.ds(pl.multiple_of((first + i) * TILE, TILE), TILE)
        images = jnp.concatenate([image_ref[at, :], other_ref[at, :]], axis=1)
        for part in range(2):
            total[part] += lax.dot_general(
                left_of(part, mine), images, (((0,), (0,)), ((), ())), preferred_element_type=jnp.float32
            )
        return carry

    lax.fori_loop(0, count, tile, 0)


def combine(mixed, total, width):
    chunks, each2, _ = mixed.shape
    each = each2 // 2
    for t in range(2):
        re = slice(2 * t * width, (2 * t + 1) * width)
        im = slice((2 * t + 1) * width, (2 * t + 2) * width)
        to = slice(t * width, (t + 1) * width)
        real = total[0, :, re] + total[1, :, im]
        imag = total[0, :, im] - total[1, :, re]
        mixed[:, :each, to] = real.reshape(chunks, each, width)
        mixed[:, each:, to] = imag.reshape(chunks, each, width)


def near_kernel(left_ref, image_ref, other_ref, out_ref, total):
    total[...] = jnp.zeros_like(total)
    add_tiles(total, lambda p, at: left_ref[p, at, :], image_ref, other_ref, 0, left_ref.shape[1] // TILE)
    combine(out_ref, total, left_ref.shape[-1])


def tail_kernel(tail0_ref, tail1_ref, image_ref, other_ref, total):
    total[...] = jnp.zeros_like(total)
    first = image_ref.shape[0] // TILE - TAIL_TILES
    tail = lambda p, at: tail0_ref[p, at, :] + tail1_ref[p, at, :]
    add_tiles(total, tail, image_ref, other_ref, first, TAIL_TILES)


def far_kernel(left_ref, image_ref, other_ref, tail_ref, near_ref, out_ref, total, mixed):
    total[...] = tail_ref[...]
    add_tiles(total, lambda p, at: left_ref[p, at, :], image_ref, other_ref, 0, left_ref.shape[1] // TILE)
    combine(mixed, total, left_ref.shape[-1])
    out_ref[...] = jnp.concatenate([near_ref[...], mixed[...]], axis=1).astype(out_ref.dtype)


def project(kernel, out, scratch, *args):
    vmem = pl.BlockSpec(memory_space=pltpu.VMEM)
    return pl.pallas_call(
        kernel,
        out_shape=out,
        in_specs=[vmem] * len(args),
        out_specs=vmem,
        scratch_shapes=[pltpu.VMEM(shape, jnp.float32) for shape in scratch],
        compiler_params=pltpu.CompilerParams(vmem_limit_bytes=12 * 1024 * 1024),
        cost_estimate=pl.CostEstimate(flops=500_000_000, bytes_accessed=3_500_000, transcendentals=0),
    )(*args)


def local(right_vecs, left_vecs, dip_blocks, block_cols, block_counts):
    parts, span, width = right_vecs.shape
    blocks, _, _, size, _ = dip_blocks.shape
    n_rows = lax.axis_size("rows")
    n_cols = lax.axis_size("cols")
    each = width // n_rows
    forward = [(i, i + 1) for i in range(n_rows - 1)]
    backward = [(j, i) for i, j in forward]
    blocked = lambda x: x.reshape(parts, blocks, size, width)
    local_cols = block_cols - (lax.axis_index("rows") - 1) * blocks
    low = lax.ppermute(right_vecs, "rows", forward)
    high = lax.ppermute(right_vecs, "rows", backward)
    split = span - TAIL_TILES * TILE
    main, tail = left_vecs[:, :split], left_vecs[:, split:]
    inner = [(r, 0 < r % LINE < LINE - 1) for r in range(n_rows)]
    out_of = {r: r + 1 if r % LINE == 0 else r - 1 for r, inside in inner if not inside}
    flat = lambda rows: [(r * n_cols + c, r * n_cols + (c ^ 2)) for r in rows for c in range(n_cols)]
    moved = lax.ppermute(tail, "rows", list(out_of.items()))
    moved = lax.ppermute(moved, ("rows", "cols"), flat(out_of.values()))
    across = lax.ppermute(main, "cols", [(i, i ^ 2) for i in range(n_cols)])
    tail_own = lax.ppermute(tail, ("rows", "cols"), flat([r for r, inside in inner if inside]))
    tail_back = lax.ppermute(moved, "rows", [(j, i) for i, j in out_of.items()])
    acc, low_list, low_count, high_list, high_count = own_products(
        local_cols, block_counts, blocked(right_vecs), dip_blocks
    )
    acc = side_products(high_list, high_count, blocked(high), dip_blocks, acc, False)
    image = side_products(low_list, low_count, blocked(low), dip_blocks, acc, True)
    image = image.reshape(span, 2 * width)
    other = lax.ppermute(image, "cols", [(i, i ^ 1) for i in range(n_cols)])
    half = (n_rows, 2 * each, 2 * width)
    products = (2, width, 4 * width)
    near = project(near_kernel, jax.ShapeDtypeStruct(half, jnp.float32), [products], left_vecs, image, other)
    tail_sum = project(tail_kernel, jax.ShapeDtypeStruct(products, jnp.float32), [], tail_own, tail_back, image, other)
    partial = project(
        far_kernel,
        jax.ShapeDtypeStruct((n_rows, 4 * each, 2 * width), jnp.bfloat16),
        [products, half],
        across,
        image,
        other,
        tail_sum,
        near,
    )
    me = lax.axis_index("cols")
    partial, swap_left, swap_right = lax.optimization_barrier((partial, (me & 2) > 0, (me & 1) > 0))
    received = lax.all_to_all(partial, "rows", 0, 0, tiled=True)
    share = jnp.sum(received.astype(jnp.float32), axis=0)
    share = share.reshape(2, parts, each, 2, width)
    share = jnp.where(swap_left, share[::-1], share)
    share = jnp.where(swap_right, share[:, :, :, ::-1], share)
    out = lax.all_gather(share.reshape(2 * parts * each, 2 * width), "cols", axis=0)
    out = out.reshape(2, 2, 2, parts, each, 2, width)
    return out.transpose(2, 1, 4, 3, 0, 5, 6).reshape(n_cols, each, parts, n_cols * width)


def solution(mesh):
    in_specs = (
        P(None, "rows", "cols"),
        P(None, "rows", "cols"),
        P("rows", None, None, None, None),
        P("rows", None),
        P("rows"),
    )
    out_specs = P(None, "rows", None, None)
    return jax.shard_map(local, mesh=mesh, in_specs=in_specs, out_specs=out_specs, check_vma=False)
```
